32 devices in a mesh: row: 8 (over z, x), col: 4 (over y, core).
Axes of the slice: x: 2, y: 2, z: 4, core: 2. Of those that a mesh axis runs over, the one named last changes fastest.
Arguments:
- matrix: float32 [16384, 16384], P('row', 'col'), may hold values from -300 to 300, as said below
Outputs:
- trailing: float32 [16384, 16384], P('row', 'col')
- reflectors: float32 [16384, 8], P('row')
The draws below stay inside these ranges and needn't reach their ends.
Inputs may be any that keep to these rules, and one draw needn't show every extreme that they name: matrix is exactly symmetric.
All inputs are finite; a program needn't handle non-finite values.
Results may differ from the reference program's by a relative error of at most 0.00021.
Values sent between devices are 32-bit elements; how exact they have to be, the bound alone decides.
A program may use at most 128 MiB of HBM per device.

```python
import math
import jax
import jax.numpy as jnp
from jax import lax

N = 16384
COLS = 8


def draw_matrix(key, part):
    first_key, second_key = jax.random.split(jax.random.fold_in(key, 11))
    positions = jnp.arange(N, dtype=jnp.float32)
    rising = jnp.exp(0.5 * math.log(3.0) * positions / N)
    entries = jnp.clip(jax.random.normal(first_key, (N, N), jnp.float32), -6.0, 6.0)
    spread = jnp.exp(0.5 * jax.random.uniform(second_key, (N,), jnp.float32, 0.0, math.log(10.0)))
    symmetric = (entries + entries.T) * (1.0 / math.sqrt(2.0))
    scales = rising * spread
    outer = scales[:, None] * scales[None, :]
    return (symmetric * outer).astype(jnp.float32)


def setup_inputs(seed: int = 0) -> dict:
    streams_of = jax.random.split(jax.random.key(seed), 2)
    return {
        "matrix": draw_matrix(jax.random.fold_in(streams_of[1], 71), 0),
    }


def precise_dot(operand, factor):
    return jnp.dot(operand, factor, precision=lax.Precision.HIGHEST, preferred_element_type=jnp.float32)

def reference(matrix):
    reflect = jnp.zeros((N, COLS), jnp.float32)
    companion = jnp.zeros((N, COLS), jnp.float32)
    positions = jnp.arange(N, dtype=jnp.int32)
    for column in range(COLS):
        current = matrix[:, column] - precise_dot(reflect, companion[column]) - precise_dot(companion, reflect[column])
        below_part = jnp.where(positions > column, current, 0.0)
        squared = jnp.sum(below_part * below_part)
        leading = jnp.sum(jnp.where(positions == column + 1, current, 0.0))
        length = jnp.sqrt(squared)
        vector = below_part + jnp.where(positions == column + 1, length, 0.0)
        scaling = 1.0 / (length * (length + leading))
        column_image = precise_dot(matrix, vector)
        weight_comp = precise_dot(companion.T, vector)
        weight_refl = precise_dot(reflect.T, vector)
        pushed = scaling * (column_image - precise_dot(reflect, weight_comp) - precise_dot(companion, weight_refl))
        inner_product = jnp.sum(pushed * vector)
        update = pushed - 0.5 * scaling * inner_product * vector
        reflect = reflect.at[:, column].set(vector)
        companion = companion.at[:, column].set(update)
    trailing = matrix - precise_dot(reflect, companion.T) - precise_dot(companion, reflect.T)
    return (trailing, reflect)
```

```python
import functools

import jax
import jax.numpy as jnp
from jax import lax
from jax.experimental import pallas as pl
from jax.experimental.pallas import tpu as pltpu
from jax.sharding import PartitionSpec as P

COLS = 8
LANES = 128
MESH = pl.DeviceIdType.MESH

def from_root(block, axis, source):
    block = jnp.where(lax.axis_index(axis) == source, block, jnp.zeros_like(block))
    return lax.psum(block, axis)


def precise_dot(operand, factor):
    return jnp.dot(
        operand, factor, precision=lax.Precision.HIGHEST, preferred_element_type=jnp.float32
    )


def local_general(matrix):
    rows_local = matrix.shape[0]
    cols_local = matrix.shape[1]
    row_index = lax.axis_index("row")
    col_index = lax.axis_index("col")
    panel = from_root(matrix[:, :COLS], "col", 0)
    whole_panel = lax.all_gather(panel, "row", axis=0, tiled=True)
    all_ids = jnp.arange(whole_panel.shape[0], dtype=jnp.int32)
    reflect = jnp.zeros((all_ids.shape[0], COLS), jnp.float32)
    companion = jnp.zeros((all_ids.shape[0], COLS), jnp.float32)
    for column in range(COLS):
        reflect_rows = lax.dynamic_slice_in_dim(reflect, row_index * rows_local, rows_local, 0)
        companion_rows = lax.dynamic_slice_in_dim(companion, row_index * rows_local, rows_local, 0)
        current = (
            whole_panel[:, column]
            - precise_dot(reflect, companion[column])
            - precise_dot(companion, reflect[column])
        )
        below_whole = jnp.where(all_ids > column, current, 0.0)
        squared = jnp.sum(below_whole * below_whole)
        leading = jnp.sum(jnp.where(all_ids == column + 1, current, 0.0))
        length = jnp.sqrt(squared)
        vector = below_whole + jnp.where(all_ids == column + 1, length, 0.0)
        scaling = 1.0 / (length * (length + leading))
        vector_rows = lax.dynamic_slice_in_dim(vector, row_index * rows_local, rows_local, 0)
        vector_cols = lax.dynamic_slice_in_dim(vector, col_index * cols_local, cols_local, 0)
        weight_comp = precise_dot(companion.T, vector)
        weight_refl = precise_dot(reflect.T, vector)
        row_image = lax.psum(precise_dot(matrix, vector_cols), "col")
        pushed = scaling * (
            row_image
            - precise_dot(reflect_rows, weight_comp)
            - precise_dot(companion_rows, weight_refl)
        )
        inner_product = lax.psum(jnp.sum(pushed * vector_rows), "row")
        update_rows = pushed - 0.5 * scaling * inner_product * vector_rows
        update = lax.all_gather(update_rows, "row", axis=0, tiled=True)
        reflect = reflect.at[:, column].set(vector)
        companion = companion.at[:, column].set(update)
    reflect_rows = lax.dynamic_slice_in_dim(reflect, row_index * rows_local, rows_local, 0)
    companion_rows = lax.dynamic_slice_in_dim(companion, row_index * rows_local, rows_local, 0)
    reflect_cols = lax.dynamic_slice_in_dim(reflect, col_index * cols_local, cols_local, 0)
    companion_cols = lax.dynamic_slice_in_dim(companion, col_index * cols_local, cols_local, 0)
    trailing = (
        matrix
        - precise_dot(reflect_rows, companion_cols.T)
        - precise_dot(companion_rows, reflect_cols.T)
    )
    return (trailing, reflect_rows)


def total(values):
    folded = jnp.sum(values, axis=0)
    return jnp.sum(jnp.sum(folded, axis=0, keepdims=True), axis=1, keepdims=True)


def pick(values, chosen):
    kept = jnp.where(chosen, values, 0.0)
    return jnp.sum(jnp.sum(kept, axis=0, keepdims=True), axis=1, keepdims=True)


def panel_kernel(
    nr, nc, a_hbm, left_ref, right_ref,
    a, raw, mine, panel, acc, part, arrived, image, vecs, comps, nxt, corr,
    load_sem, scatter_sem, raw_sem, psend_sem, precv_sem,
    send1_sem, recv1_sem, send2_sem, recv2_sem,
):
    r = lax.axis_index("row")
    c = lax.axis_index("col")
    n = nr * nc
    rows, cols = a.shape
    quarter = rows // nc
    width = cols // nr
    subs = quarter // LANES
    tiles = cols // LANES
    here = r * nc + c

    def flip(t):
        return t + 1 - 2 * lax.rem(t, 2)

    def turn(i):
        t = lax.rem(c + 2 * (nc // 2 - 1 - i // 2), nc)
        own = i >= nc - 2
        second = lax.rem(i, 2) == 1
        first_of = jnp.where(own, flip(c), t)
        second_of = jnp.where(own, c, flip(t))
        return jnp.where(second, second_of, first_of)

    def load(i):
        at = pl.ds(pl.multiple_of(turn(i) * quarter, quarter), quarter)
        return pltpu.make_async_copy(a_hbm.at[at], a.at[at], load_sem.at[i])

    def rowcopy(q):
        at = pl.ds(pl.multiple_of(q * width, width), width)
        return a_hbm.at[pl.ds(0, COLS), at]

    @pl.when(r == 0)
    def _():
        pltpu.make_async_copy(rowcopy(0), raw, raw_sem).start()

    for i in range(nc):
        load(i).start()

    barrier = pltpu.get_barrier_semaphore()

    def greet(d, carry):
        t = lax.rem(here + d, n)
        pl.semaphore_signal(barrier, inc=1, device_id=(t // nc, lax.rem(t, nc)), device_id_type=MESH)
        return carry

    lax.fori_loop(1, n, greet, 0)

    def clear(k, carry):
        vecs[k] = jnp.zeros(vecs.shape[1:], jnp.float32)
        comps[k] = jnp.zeros(comps.shape[1:], jnp.float32)
        return carry

    lax.fori_loop(0, COLS + 1, clear, 0)
    pl.semaphore_wait(barrier, n - 1)

    def scatter(q):
        return pltpu.make_async_remote_copy(
            src_ref=rowcopy(q), dst_ref=raw, send_sem=scatter_sem.at[q], recv_sem=raw_sem,
            device_id=(q, c), device_id_type=MESH,
        )

    @pl.when(r == 0)
    def _():
        for q in range(1, nr):
            scatter(q).start()

    pltpu.make_async_copy(raw, raw, raw_sem).wait()
    for k in range(COLS):
        for m in range(subs):
            mine[k, m : m + 1, :] = raw[k : k + 1, m * LANES : (m + 1) * LANES]
    spot = c * nr + r
    panel[spot] = mine[...]

    def spread(d, carry):
        t = lax.rem(here + d, n)
        pltpu.make_async_remote_copy(
            src_ref=mine, dst_ref=panel.at[spot], send_sem=psend_sem, recv_sem=precv_sem,
            device_id=(t // nc, lax.rem(t, nc)), device_id_type=MESH,
        ).start()
        return carry

    lax.fori_loop(1, n, spread, 0)
    most = panel.at[pl.ds(0, n - 1)]
    pltpu.make_async_copy(most, most, precv_sem).wait()
    pltpu.make_async_copy(most, most, psend_sem).wait()

    @pl.when(r == 0)
    def _():
        for q in range(1, nr):
            scatter(q).wait_send()

    ids = lax.broadcasted_iota(jnp.int32, (subs, LANES), 0) * LANES + lax.broadcasted_iota(
        jnp.int32, (subs, LANES), 1
    )

    def reflect(column, current):
        vecs[column] = current
        head = jnp.where(ids > column, current[0], 0.0)
        vecs[column, 0] = head
        below = vecs[column]
        squared = total(below * below)
        leading = pick(head, ids == column + 1)
        length = jnp.sqrt(squared)
        vecs[column, 0] = head + jnp.where(ids == column + 1, length, 0.0)
        return 1.0 / (length * (length + leading))

    def step(j, scaling):
        vrows = [
            jnp.broadcast_to(vecs[j, c * nr + t // subs, t % subs : t % subs + 1, :], (8, LANES))
            for t in range(tiles)
        ]

        def block(i, carry):
            k = turn(i)

            @pl.when(j == 0)
            def _():
                load(i).wait()

            def group(g, inner):
                at = pl.ds(pl.multiple_of(k * quarter + g * 8, 8), 8)
                sums = [None] * 4
                for t in range(tiles):
                    term = a[at, t * LANES : (t + 1) * LANES] * vrows[t]
                    sums[t % 4] = term if sums[t % 4] is None else sums[t % 4] + term
                acc[pl.ds(pl.multiple_of(g * 8, 8), 8), :] = (sums[0] + sums[1]) + (sums[2] + sums[3])
                return inner

            lax.fori_loop(0, quarter // 8, group, 0, unroll=4)
            for m in range(subs):
                turned = acc[m * LANES : (m + 1) * LANES, :].T
                part[k, m : m + 1, :] = jnp.sum(turned, axis=0, keepdims=True)

            @pl.when(i < nc - 1)
            def _():
                first(k).start()

            return carry

        def first(k):
            return pltpu.make_async_remote_copy(
                src_ref=part.at[k], dst_ref=arrived.at[c], send_sem=send1_sem.at[k],
                recv_sem=recv1_sem.at[c], device_id=(r, k), device_id_type=MESH,
            )

        lax.fori_loop(0, nc, block, 0)
        value = part[c]

        def collect(d, value):
            k = lax.rem(c + d, nc)
            pltpu.make_async_copy(arrived.at[k], arrived.at[k], recv1_sem.at[k]).wait()
            return value + arrived[k]

        value = lax.fori_loop(1, nc, collect, value, unroll=True)
        image[j, here] = value

        def second(d, carry):
            t = lax.rem(here + d, n)
            pltpu.make_async_remote_copy(
                src_ref=image.at[j, here], dst_ref=image.at[j, here], send_sem=send2_sem,
                recv_sem=recv2_sem.at[j], device_id=(t // nc, lax.rem(t, nc)), device_id_type=MESH,
            ).start()
            return carry

        lax.fori_loop(1, n, second, 0, unroll=True)

        vector = vecs[j]
        corr[...] = jnp.zeros(corr.shape, jnp.float32)
        follow = jnp.minimum(j + 1, COLS - 1)
        nxt[...] = panel[:, follow]
        target = ids == j + 1

        def history(k, carry):
            v_k = vecs[k]
            w_k = comps[k]
            corr[...] = corr[...] + v_k * total(w_k * vecs[j]) + w_k * total(v_k * vecs[j])
            nxt[...] = nxt[...] - v_k * pick(w_k[0], target) - w_k * pick(v_k[0], target)
            return carry

        lax.fori_loop(0, j, history, 0)

        def sent(d, carry):
            k = lax.rem(c + d, nc)
            pltpu.make_async_copy(part.at[k], part.at[k], send1_sem.at[k]).wait()
            return carry

        lax.fori_loop(1, nc, sent, 0)
        rest = image.at[j, pl.ds(0, n - 1)]
        pltpu.make_async_copy(rest, rest, send2_sem).wait()
        pltpu.make_async_copy(rest, rest, recv2_sem.at[j]).wait()

        pushed = scaling * (image[j] - corr[...])
        inner_product = total(pushed * vector)
        update = pushed - (0.5 * scaling * inner_product) * vector
        comps[j] = update
        current = nxt[...] - vector * pick(update[0], target) - update * pick(vector[0], target)
        return reflect(j + 1, current)

    lax.fori_loop(0, COLS, step, reflect(0, panel[:, 0]))

    def place(dest, base, count):
        def move(p, carry):
            for m in range(subs):
                at = pl.ds(pl.multiple_of((p * subs + m) * LANES, LANES), LANES)
                for k in range(COLS):
                    dest[k : k + 1, at] = vecs[k, base + p, m : m + 1, :]
                    dest[COLS + k : COLS + k + 1, at] = comps[k, base + p, m : m + 1, :]
            return carry

        lax.fori_loop(0, count, move, 0)

    place(left_ref, r * nc, nc)
    place(right_ref, c * nr, nr)


def panel_call(nr, nc, matrix):
    rows, cols = matrix.shape
    n = nr * nc
    subs = rows // nc // LANES
    vector = (n, subs, LANES)
    f32 = jnp.float32
    vmem = pl.BlockSpec(memory_space=pltpu.VMEM)
    dma = pltpu.SemaphoreType.DMA
    return pl.pallas_call(
        functools.partial(panel_kernel, nr, nc),
        out_shape=(
            jax.ShapeDtypeStruct((2 * COLS, rows), f32),
            jax.ShapeDtypeStruct((2 * COLS, cols), f32),
        ),
        in_specs=[pl.BlockSpec(memory_space=pl.ANY)],
        out_specs=(vmem, vmem),
        scratch_shapes=[
            pltpu.VMEM((rows, cols), f32),
            pltpu.VMEM((COLS, cols // nr), f32),
            pltpu.VMEM((COLS, subs, LANES), f32),
            pltpu.VMEM((n, COLS, subs, LANES), f32),
            pltpu.VMEM((rows // nc, LANES), f32),
            pltpu.VMEM((nc, subs, LANES), f32),
            pltpu.VMEM((nc, subs, LANES), f32),
            pltpu.VMEM((COLS,) + vector, f32),
            pltpu.VMEM((COLS + 1,) + vector, f32),
            pltpu.VMEM((COLS + 1,) + vector, f32),
            pltpu.VMEM(vector, f32),
            pltpu.VMEM(vector, f32),
            dma((nc,)), dma((nr,)), dma, dma, dma,
            dma((nc,)), dma((nc,)), dma, dma((COLS,)),
        ],
        compiler_params=pltpu.CompilerParams(
            collective_id=0, has_side_effects=True, vmem_limit_bytes=56 * 1024 * 1024
        ),
    )(matrix)


def thirds(values):
    high = values.astype(jnp.bfloat16)
    rest = values - high.astype(jnp.float32)
    middle = rest.astype(jnp.bfloat16)
    low = (rest - middle.astype(jnp.float32)).astype(jnp.bfloat16)
    return high, middle, low


def trailing_kernel(left_ref, right_ref, a_ref, out_ref, refl_ref, stacked):
    @pl.when(pl.program_id(0) == 0)
    def _():
        swapped = jnp.concatenate([right_ref[COLS:, :], right_ref[:COLS, :]], axis=0)
        h, m, l = thirds(swapped)
        stacked[...] = jnp.concatenate([h, m, h, m, l, h], axis=0)

    left = left_ref[...]
    h, m, l = thirds(left)
    other = jnp.concatenate([h, h, m, m, h, l], axis=0)
    product = lax.dot_general(
        other, stacked[...], (((0,), (0,)), ((), ())), preferred_element_type=jnp.float32
    )
    out_ref[...] = a_ref[...] - product
    refl_ref[...] = left[:COLS, :].T


def trailing_call(left, right, matrix):
    rows, cols = matrix.shape
    tile = 128
    return pl.pallas_call(
        trailing_kernel,
        grid=(rows // tile,),
        out_shape=(
            jax.ShapeDtypeStruct((rows, cols), jnp.float32),
            jax.ShapeDtypeStruct((rows, COLS), jnp.float32),
        ),
        in_specs=[
            pl.BlockSpec((2 * COLS, tile), lambda i: (0, i)),
            pl.BlockSpec((2 * COLS, cols), lambda i: (0, 0)),
            pl.BlockSpec((tile, cols), lambda i: (i, 0)),
        ],
        out_specs=(
            pl.BlockSpec((tile, cols), lambda i: (i, 0)),
            pl.BlockSpec((tile, COLS), lambda i: (i, 0)),
        ),
        scratch_shapes=[pltpu.VMEM((12 * COLS, cols), jnp.bfloat16)],
        compiler_params=pltpu.CompilerParams(
            dimension_semantics=("arbitrary",), vmem_limit_bytes=48 * 1024 * 1024
        ),
    )(left, right, matrix)


def local(nr, nc, matrix):
    rows, cols = matrix.shape
    piece = rows // nc
    if piece % LANES or piece > 8 * LANES or cols // nr != piece or nc % 2 or nr < 2:
        return local_general(matrix)
    left, right = panel_call(nr, nc, matrix)
    return trailing_call(left, right, matrix)


def solution(mesh):
    return jax.shard_map(
        functools.partial(local, mesh.shape["row"], mesh.shape["col"]),
        mesh=mesh,
        in_specs=(P("row", "col"),),
        out_specs=(P("row", "col"), P("row", None)),
        check_vma=False,
    )
```

```python
import functools

import jax
import jax.numpy as jnp
from jax import lax
from jax.experimental import pallas as pl
from jax.experimental.pallas import tpu as pltpu
from jax.sharding import PartitionSpec as P

COLS = 8
LANES = 128
MESH = pl.DeviceIdType.MESH

def from_root(block, axis, source):
    block = jnp.where(lax.axis_index(axis) == source, block, jnp.zeros_like(block))
    return lax.psum(block, axis)


def precise_dot(operand, factor):
    return jnp.dot(
        operand, factor, precision=lax.Precision.HIGHEST, preferred_element_type=jnp.float32
    )


def local_general(matrix):
    rows_local = matrix.shape[0]
    cols_local = matrix.shape[1]
    row_index = lax.axis_index("row")
    col_index = lax.axis_index("col")
    panel = from_root(matrix[:, :COLS], "col", 0)
    whole_panel = lax.all_gather(panel, "row", axis=0, tiled=True)
    all_ids = jnp.arange(whole_panel.shape[0], dtype=jnp.int32)
    reflect = jnp.zeros((all_ids.shape[0], COLS), jnp.float32)
    companion = jnp.zeros((all_ids.shape[0], COLS), jnp.float32)
    for column in range(COLS):
        reflect_rows = lax.dynamic_slice_in_dim(reflect, row_index * rows_local, rows_local, 0)
        companion_rows = lax.dynamic_slice_in_dim(companion, row_index * rows_local, rows_local, 0)
        current = (
            whole_panel[:, column]
            - precise_dot(reflect, companion[column])
            - precise_dot(companion, reflect[column])
        )
        below_whole = jnp.where(all_ids > column, current, 0.0)
        squared = jnp.sum(below_whole * below_whole)
        leading = jnp.sum(jnp.where(all_ids == column + 1, current, 0.0))
        length = jnp.sqrt(squared)
        vector = below_whole + jnp.where(all_ids == column + 1, length, 0.0)
        scaling = 1.0 / (length * (length + leading))
        vector_rows = lax.dynamic_slice_in_dim(vector, row_index * rows_local, rows_local, 0)
        vector_cols = lax.dynamic_slice_in_dim(vector, col_index * cols_local, cols_local, 0)
        weight_comp = precise_dot(companion.T, vector)
        weight_refl = precise_dot(reflect.T, vector)
        row_image = lax.psum(precise_dot(matrix, vector_cols), "col")
        pushed = scaling * (
            row_image
            - precise_dot(reflect_rows, weight_comp)
            - precise_dot(companion_rows, weight_refl)
        )
        inner_product = lax.psum(jnp.sum(pushed * vector_rows), "row")
        update_rows = pushed - 0.5 * scaling * inner_product * vector_rows
        update = lax.all_gather(update_rows, "row", axis=0, tiled=True)
        reflect = reflect.at[:, column].set(vector)
        companion = companion.at[:, column].set(update)
    reflect_rows = lax.dynamic_slice_in_dim(reflect, row_index * rows_local, rows_local, 0)
    companion_rows = lax.dynamic_slice_in_dim(companion, row_index * rows_local, rows_local, 0)
    reflect_cols = lax.dynamic_slice_in_dim(reflect, col_index * cols_local, cols_local, 0)
    companion_cols = lax.dynamic_slice_in_dim(companion, col_index * cols_local, cols_local, 0)
    trailing = (
        matrix
        - precise_dot(reflect_rows, companion_cols.T)
        - precise_dot(companion_rows, reflect_cols.T)
    )
    return (trailing, reflect_rows)


def total(values):
    folded = jnp.sum(values, axis=0)
    return jnp.sum(jnp.sum(folded, axis=0, keepdims=True), axis=1, keepdims=True)


def pick(values, chosen):
    kept = jnp.where(chosen, values, 0.0)
    return jnp.sum(jnp.sum(kept, axis=0, keepdims=True), axis=1, keepdims=True)


def panel_kernel(
    nr, nc, a_hbm, left_ref, right_ref, a,
    raw, mine, panel, acc, part, arrived, image, vecs, comps, nxt, corr,
    load_sem, scatter_sem, raw_sem, psend_sem, precv_sem,
    send1_sem, recv1_sem, send2_sem, recv2_sem,
):
    r = lax.axis_index("row")
    c = lax.axis_index("col")
    n = nr * nc
    rows, cols = a.shape
    quarter = rows // nc
    width = cols // nr
    subs = quarter // LANES
    tiles = cols // LANES
    here = r * nc + c

    def flip(t):
        return t + 1 - 2 * lax.rem(t, 2)

    def turn(i):
        t = lax.rem(c + 2 * (nc // 2 - 1 - i // 2), nc)
        own = i >= nc - 2
        second = lax.rem(i, 2) == 1
        first_of = jnp.where(own, flip(c), t)
        second_of = jnp.where(own, c, flip(t))
        return jnp.where(second, second_of, first_of)

    def load(i):
        at = pl.ds(pl.multiple_of(turn(i) * quarter, quarter), quarter)
        return pltpu.make_async_copy(a_hbm.at[at], a.at[at], load_sem.at[i])

    def rowcopy(q):
        at = pl.ds(pl.multiple_of(q * width, width), width)
        return a_hbm.at[pl.ds(0, COLS), at]

    @pl.when(r == 0)
    def _():
        pltpu.make_async_copy(rowcopy(0), raw, raw_sem).start()

    for i in range(nc):
        load(i).start()

    barrier = pltpu.get_barrier_semaphore()

    def greet(d, carry):
        t = lax.rem(here + d, n)
        pl.semaphore_signal(barrier, inc=1, device_id=(t // nc, lax.rem(t, nc)), device_id_type=MESH)
        return carry

    lax.fori_loop(1, n, greet, 0)

    def clear(k, carry):
        vecs[k] = jnp.zeros(vecs.shape[1:], jnp.float32)
        comps[k] = jnp.zeros(comps.shape[1:], jnp.float32)
        return carry

    lax.fori_loop(0, COLS + 1, clear, 0)
    pl.semaphore_wait(barrier, n - 1)

    def scatter(q):
        return pltpu.make_async_remote_copy(
            src_ref=rowcopy(q), dst_ref=raw, send_sem=scatter_sem.at[q], recv_sem=raw_sem,
            device_id=(q, c), device_id_type=MESH,
        )

    @pl.when(r == 0)
    def _():
        for q in range(1, nr):
            scatter(q).start()

    pltpu.make_async_copy(raw, raw, raw_sem).wait()
    for k in range(COLS):
        for m in range(subs):
            mine[k, m : m + 1, :] = raw[k : k + 1, m * LANES : (m + 1) * LANES]
    spot = c * nr + r
    panel[spot] = mine[...]

    def spread(d, carry):
        t = lax.rem(here + d, n)
        pltpu.make_async_remote_copy(
            src_ref=mine, dst_ref=panel.at[spot], send_sem=psend_sem, recv_sem=precv_sem,
            device_id=(t // nc, lax.rem(t, nc)), device_id_type=MESH,
        ).start()
        return carry

    lax.fori_loop(1, n, spread, 0)
    most = panel.at[pl.ds(0, n - 1)]
    pltpu.make_async_copy(most, most, precv_sem).wait()
    pltpu.make_async_copy(most, most, psend_sem).wait()

    @pl.when(r == 0)
    def _():
        for q in range(1, nr):
            scatter(q).wait_send()

    ids = lax.broadcasted_iota(jnp.int32, (subs, LANES), 0) * LANES + lax.broadcasted_iota(
        jnp.int32, (subs, LANES), 1
    )

    def reflect(column, current):
        vecs[column] = current
        head = jnp.where(ids > column, current[0], 0.0)
        vecs[column, 0] = head
        below = vecs[column]
        squared = total(below * below)
        leading = pick(head, ids == column + 1)
        length = jnp.sqrt(squared)
        vecs[column, 0] = head + jnp.where(ids == column + 1, length, 0.0)
        return 1.0 / (length * (length + leading))

    def step(j, scaling):
        vrows = [
            jnp.broadcast_to(vecs[j, c * nr + t // subs, t % subs : t % subs + 1, :], (8, LANES))
            for t in range(tiles)
        ]

        def block(i, carry):
            k = turn(i)

            @pl.when(j == 0)
            def _():
                load(i).wait()

            def group(g, inner):
                at = pl.ds(pl.multiple_of(k * quarter + g * 8, 8), 8)
                sums = [None] * 4
                for t in range(tiles):
                    term = a[at, t * LANES : (t + 1) * LANES] * vrows[t]
                    sums[t % 4] = term if sums[t % 4] is None else sums[t % 4] + term
                acc[pl.ds(pl.multiple_of(g * 8, 8), 8), :] = (sums[0] + sums[1]) + (sums[2] + sums[3])
                return inner

            lax.fori_loop(0, quarter // 8, group, 0, unroll=16)
            for m in range(subs):
                turned = acc[m * LANES : (m + 1) * LANES, :].T
                part[k, m : m + 1, :] = jnp.sum(turned, axis=0, keepdims=True)

            @pl.when(i < nc - 1)
            def _():
                first(k).start()

            return carry

        def first(k):
            return pltpu.make_async_remote_copy(
                src_ref=part.at[k], dst_ref=arrived.at[c], send_sem=send1_sem.at[k],
                recv_sem=recv1_sem.at[c], device_id=(r, k), device_id_type=MESH,
            )

        lax.fori_loop(0, nc, block, 0)
        value = part[c]

        def collect(d, value):
            k = lax.rem(c + d, nc)
            pltpu.make_async_copy(arrived.at[k], arrived.at[k], recv1_sem.at[k]).wait()
            return value + arrived[k]

        value = lax.fori_loop(1, nc, collect, value, unroll=True)
        image[j, here] = value

        def second(d, carry):
            t = lax.rem(here + d, n)
            pltpu.make_async_remote_copy(
                src_ref=image.at[j, here], dst_ref=image.at[j, here], send_sem=send2_sem,
                recv_sem=recv2_sem.at[j], device_id=(t // nc, lax.rem(t, nc)), device_id_type=MESH,
            ).start()
            return carry

        for d in sorted(range(1, n), key=lambda d: abs(d - n // 2)):
            second(d, 0)

        vector = vecs[j]
        corr[...] = jnp.zeros(corr.shape, jnp.float32)
        follow = jnp.minimum(j + 1, COLS - 1)
        nxt[...] = panel[:, follow]
        target = ids == j + 1

        def history(k, carry):
            v_k = vecs[k]
            w_k = comps[k]
            corr[...] = corr[...] + v_k * total(w_k * vecs[j]) + w_k * total(v_k * vecs[j])
            nxt[...] = nxt[...] - v_k * pick(w_k[0], target) - w_k * pick(v_k[0], target)
            return carry

        lax.fori_loop(0, j, history, 0)

        def sent(d, carry):
            k = lax.rem(c + d, nc)
            pltpu.make_async_copy(part.at[k], part.at[k], send1_sem.at[k]).wait()
            return carry

        lax.fori_loop(1, nc, sent, 0)
        rest = image.at[j, pl.ds(0, n - 1)]
        pltpu.make_async_copy(rest, rest, send2_sem).wait()
        pltpu.make_async_copy(rest, rest, recv2_sem.at[j]).wait()

        pushed = scaling * (image[j] - corr[...])
        inner_product = total(pushed * vector)
        update = pushed - (0.5 * scaling * inner_product) * vector
        comps[j] = update
        current = nxt[...] - vector * pick(update[0], target) - update * pick(vector[0], target)
        return reflect(j + 1, current)

    lax.fori_loop(0, COLS, step, reflect(0, panel[:, 0]))

    def place(dest, base, count):
        def move(p, carry):
            for m in range(subs):
                at = pl.ds(pl.multiple_of((p * subs + m) * LANES, LANES), LANES)
                for k in range(COLS):
                    dest[k : k + 1, at] = vecs[k, base + p, m : m + 1, :]
                    dest[COLS + k : COLS + k + 1, at] = comps[k, base + p, m : m + 1, :]
            return carry

        lax.fori_loop(0, count, move, 0)

    place(left_ref, r * nc, nc)
    place(right_ref, c * nr, nr)


def panel_call(nr, nc, matrix):
    rows, cols = matrix.shape
    n = nr * nc
    subs = rows // nc // LANES
    vector = (n, subs, LANES)
    f32 = jnp.float32
    vmem = pl.BlockSpec(memory_space=pltpu.VMEM)
    dma = pltpu.SemaphoreType.DMA
    return pl.pallas_call(
        functools.partial(panel_kernel, nr, nc),
        out_shape=(
            jax.ShapeDtypeStruct((2 * COLS, rows), f32),
            jax.ShapeDtypeStruct((2 * COLS, cols), f32),
            pltpu.VMEM((rows, cols), f32),
        ),
        in_specs=[pl.BlockSpec(memory_space=pl.ANY)],
        out_specs=(vmem, vmem, vmem),
        scratch_shapes=[
            pltpu.VMEM((COLS, cols // nr), f32),
            pltpu.VMEM((COLS, subs, LANES), f32),
            pltpu.VMEM((n, COLS, subs, LANES), f32),
            pltpu.VMEM((rows // nc, LANES), f32),
            pltpu.VMEM((nc, subs, LANES), f32),
            pltpu.VMEM((nc, subs, LANES), f32),
            pltpu.VMEM((COLS,) + vector, f32),
            pltpu.VMEM((COLS + 1,) + vector, f32),
            pltpu.VMEM((COLS + 1,) + vector, f32),
            pltpu.VMEM(vector, f32),
            pltpu.VMEM(vector, f32),
            dma((nc,)), dma((nr,)), dma, dma, dma,
            dma((nc,)), dma((nc,)), dma, dma((COLS,)),
        ],
        compiler_params=pltpu.CompilerParams(
            collective_id=0, has_side_effects=True, vmem_limit_bytes=8 * 1024 * 1024
        ),
    )(matrix)


def thirds(values):
    high = values.astype(jnp.bfloat16)
    rest = values - high.astype(jnp.float32)
    middle = rest.astype(jnp.bfloat16)
    low = (rest - middle.astype(jnp.float32)).astype(jnp.bfloat16)
    return high, middle, low


def trailing_kernel(left_ref, right_ref, a_ref, out_ref, refl_ref, stacked):
    @pl.when(pl.program_id(0) == 0)
    def _():
        swapped = jnp.concatenate([right_ref[COLS:, :], right_ref[:COLS, :]], axis=0)
        h, m, l = thirds(swapped)
        stacked[...] = jnp.concatenate([h, m, h, m, l, h], axis=0)

    left = left_ref[...]
    h, m, l = thirds(left)
    other = jnp.concatenate([h, h, m, m, h, l], axis=0)
    product = lax.dot_general(
        other, stacked[...], (((0,), (0,)), ((), ())), preferred_element_type=jnp.float32
    )
    at = pl.ds(pl.multiple_of(pl.program_id(0) * out_ref.shape[0], out_ref.shape[0]), out_ref.shape[0])
    out_ref[...] = a_ref[at, :] - product
    refl_ref[...] = left[:COLS, :]


def trailing_call(left, right, matrix):
    rows, cols = matrix.shape
    tile = 128
    return pl.pallas_call(
        trailing_kernel,
        grid=(rows // tile,),
        out_shape=(
            jax.ShapeDtypeStruct((rows, cols), jnp.float32),
            jax.ShapeDtypeStruct((COLS, rows), jnp.float32),
        ),
        in_specs=[
            pl.BlockSpec((2 * COLS, tile), lambda i: (0, i)),
            pl.BlockSpec((2 * COLS, cols), lambda i: (0, 0)),
            pl.BlockSpec(memory_space=pltpu.VMEM),
        ],
        out_specs=(
            pl.BlockSpec((tile, cols), lambda i: (i, 0)),
            pl.BlockSpec((COLS, tile), lambda i: (0, i)),
        ),
        scratch_shapes=[pltpu.VMEM((12 * COLS, cols), jnp.bfloat16)],
        compiler_params=pltpu.CompilerParams(
            dimension_semantics=("arbitrary",), vmem_limit_bytes=16 * 1024 * 1024
        ),
    )(left, right, matrix)


def local(nr, nc, matrix):
    rows, cols = matrix.shape
    piece = rows // nc
    if piece % LANES or piece > 8 * LANES or cols // nr != piece or nc % 2 or nr < 2:
        return local_general(matrix)
    left, right, kept = panel_call(nr, nc, matrix)
    trailing, reflectors = trailing_call(left, right, kept)
    return trailing, reflectors.T


def solution(mesh):
    return jax.shard_map(
        functools.partial(local, mesh.shape["row"], mesh.shape["col"]),
        mesh=mesh,
        in_specs=(P("row", "col"),),
        out_specs=(P("row", "col"), P("row", None)),
        check_vma=False,
    )
```
